32 devices in a mesh: oi: 4 (over y, x), oj: 8 (over z, core).
Axes of the slice: x: 2, y: 2, z: 4, core: 2. Of those that a mesh axis runs over, the one named last changes fastest.
Arguments:
- amplitudes: float32 [128, 128, 128], P(('oi', 'oj')), may hold values from -4 to 4
- integrals: float32 [128, 128, 128], P(('oi', 'oj')), may hold values from -6 to 6
- pno_energy: float32 [128, 128], P(('oi', 'oj')), may hold values from 0.3 to 3
- pair_shift: float32 [128], P(('oi', 'oj')), may hold values from 0.5 to 2
- column_margin: bfloat16 [4096, 128, 128], P(('oi', 'oj')), may hold values from -0.5 to 1.8, as said below
- row_margin: bfloat16 [4096, 128, 128], P(('oi', 'oj')), may hold values from -0.5 to 1.8, as said below
- column_coupling: float32 [4096], P(('oi', 'oj')), may hold values from -0.3 to 0.3
- row_coupling: float32 [4096], P(('oi', 'oj')), may hold values from -0.3 to 0.3
- column_target: int32 [4096], P(('oi', 'oj')), may hold values from 0 to 3
- row_target: int32 [4096], P(('oi', 'oj')), may hold values from 0 to 3
- column_source: int32 [4096], P(('oi', 'oj')), may hold values from 0 to 7
- row_source: int32 [4096], P(('oi', 'oj')), may hold values from 0 to 15
- column_sends: int32 [128, 2], P(('oi', 'oj')), may hold values from 0 to 3, as said below
- row_sends: int32 [256, 2], P(('oi', 'oj')), may hold values from 0 to 3, as said below
- term_counts: int32 [32, 2], P(('oi', 'oj')), may hold values from 1 to 128, as said below
Outputs:
- updated: float32 [128, 128, 128], P(('oi', 'oj'))
- residual: float32 [128, 128, 128], P(('oi', 'oj'))
The draws below stay inside these ranges and needn't reach their ends.
Inputs may be any that keep to these rules, and one draw needn't show every extreme that they name: `column_margin`: each margin block is a 128 by 128 matrix of rank 128. `row_margin`: each margin block is a 128 by 128 matrix of rank 128. `column_sends`: each row names 2 different local pairs of its device. `row_sends`: each row names 2 different local pairs of its device. `term_counts`: some device has 128 live column terms and some device 128 live row terms.
All inputs are finite; a program needn't handle non-finite values.
Results may differ from the reference program's by a relative error of at most 0.0041.
Values may be sent and summed in bfloat16 or wider, within the bound.
A program may use at most 128 MiB of HBM per device.

```python
import math
import jax
import jax.numpy as jnp
from jax import lax

PNO = 128
PAIRS_DEV = 4
CAP = 2
TERMS_DEV = 128
ITERS = 2
PAIRS = 128
TERMS = 4096
N_OI = 4
N_OJ = 8


def margin_draw(key, term_total):
    diag_key, jitter_key = jax.random.split(key, 2)
    diagonal = jax.random.uniform(diag_key, (term_total, PNO), jnp.float32, 0.7, 1.3)
    jitter = jnp.clip(jax.random.normal(jitter_key, (term_total, PNO, PNO), jnp.float32), -4.0, 4.0)
    identity = jnp.eye(PNO, dtype=jnp.float32)[None]
    return (identity * diagonal[:, :, None] + jitter * (0.6 / math.sqrt(PNO))).astype(jnp.bfloat16)


def draw_column_margin(key, part):
    return margin_draw(jax.random.fold_in(key, 11), TERMS)


def draw_row_margin(key, part):
    return margin_draw(jax.random.fold_in(key, 23), TERMS)


def send_lists(key, row_total):
    row_keys = jax.random.split(key, row_total)
    return jax.vmap(lambda row_key: jax.random.permutation(row_key, PAIRS_DEV)[:CAP])(row_keys).astype(jnp.int32)


def draw_column_sends(key, part):
    return send_lists(jax.random.fold_in(key, 31), N_OI * N_OJ * N_OI)


def draw_row_sends(key, part):
    return send_lists(jax.random.fold_in(key, 37), N_OI * N_OJ * N_OJ)


def draw_term_counts(key, part):
    devices_total = N_OI * N_OJ
    base_key, heavy_key, pick_key = jax.random.split(jax.random.fold_in(key, 41), 3)
    base = jax.random.randint(base_key, (devices_total, 2), max(1, TERMS_DEV // 8), TERMS_DEV // 3 + 1, dtype=jnp.int32)
    heavy = jax.random.randint(heavy_key, (devices_total, 2), 0, 8, dtype=jnp.int32) == 0
    chosen = jax.random.randint(pick_key, (1, 2), 0, devices_total, dtype=jnp.int32)
    filled = heavy | (jnp.arange(devices_total, dtype=jnp.int32)[:, None] == chosen)
    return jnp.where(filled, jnp.int32(TERMS_DEV), base).astype(jnp.int32)


def place_ends(values, key, smallest, largest):
    index_at = [jax.random.randint(jax.random.fold_in(key, axis), (), 0, length) for axis, length in enumerate(values.shape)]
    main_axis = values.shape.index(max(values.shape))
    neighbour = index_at[:main_axis] + [(index_at[main_axis] + 1) % values.shape[main_axis]] + index_at[main_axis + 1:]
    return values.at[tuple(index_at)].set(smallest).at[tuple(neighbour)].set(largest)


def shard_levels(key, dims, cuts, low, top_value):
    factor_of = 1.0
    for dim, parts in cuts:
        steps = jax.random.uniform(jax.random.fold_in(jax.random.fold_in(key, 6), dim), (parts,), jnp.float32, low / len(cuts), top_value / len(cuts))
        factor_of = factor_of * jnp.repeat(jnp.exp(steps), dims[dim] // parts).reshape((-1,) + (1,) * (len(dims) - 1 - dim))
    return factor_of


def noise(key, shape, scale, limit, shards=(), held_as=jnp.bfloat16):
    array = scale * jax.random.normal(key, shape, jnp.float32)
    if shards:
        array = array * shard_levels(key, shape, shards, -0.22, 0.18)
    return jnp.clip(array, -limit, limit).astype(held_as)


def setup_inputs(seed: int = 0) -> dict:
    splits = jax.random.split(jax.random.key(seed), 16)
    amplitudes = noise(splits[0], (PAIRS, PNO, PNO), 0.5, 4.0, ((0, 32),), jnp.float32)
    integrals = noise(splits[1], (PAIRS, PNO, PNO), 1.0, 6.0, ((0, 32),), jnp.float32)
    pno_energy = jnp.clip(jnp.exp(math.log(3.0) - 2.3025851 * jax.random.uniform(splits[2], (PAIRS, PNO), jnp.float32) ** shard_levels(splits[2], (PAIRS, PNO), ((0, 32),), -0.2, 0.2)), 0.3, 3.0)
    pair_shift = jnp.clip(0.5 + 1.5 * jax.random.uniform(splits[3], (PAIRS,), jnp.float32) ** shard_levels(splits[3], (PAIRS,), ((0, 32),), -0.2, 0.2), 0.5, 2.0)
    column_margin = draw_column_margin(jax.random.fold_in(splits[15], 71), 0)
    row_margin = draw_row_margin(jax.random.fold_in(splits[15], 71), 0)
    column_coupling = jnp.clip(jax.random.uniform(splits[6], (TERMS,), jnp.float32, -0.3, 0.3) * shard_levels(splits[6], (TERMS,), ((0, 32),), -0.4, 0.0), -0.3, 0.3)
    row_coupling = jnp.clip(jax.random.uniform(splits[7], (TERMS,), jnp.float32, -0.3, 0.3) * shard_levels(splits[7], (TERMS,), ((0, 32),), -0.4, 0.0), -0.3, 0.3)
    column_target = place_ends(jax.random.randint(splits[8], (TERMS,), 0, PAIRS_DEV), jax.random.fold_in(splits[8], 1), 0, PAIRS_DEV - 1).astype(jnp.int32)
    row_target = place_ends(jax.random.randint(splits[9], (TERMS,), 0, PAIRS_DEV), jax.random.fold_in(splits[9], 1), 0, PAIRS_DEV - 1).astype(jnp.int32)
    column_source = place_ends(jax.random.randint(splits[10], (TERMS,), 0, N_OI * CAP), jax.random.fold_in(splits[10], 1), 0, (N_OI * CAP) - 1).astype(jnp.int32)
    row_source = place_ends(jax.random.randint(splits[11], (TERMS,), 0, N_OJ * CAP), jax.random.fold_in(splits[11], 1), 0, (N_OJ * CAP) - 1).astype(jnp.int32)
    column_sends = draw_column_sends(jax.random.fold_in(splits[15], 71), 0)
    row_sends = draw_row_sends(jax.random.fold_in(splits[15], 71), 0)
    term_counts = draw_term_counts(jax.random.fold_in(splits[15], 71), 0)
    return {"amplitudes": amplitudes, "integrals": integrals, "pno_energy": pno_energy, "pair_shift": pair_shift, "column_margin": column_margin, "row_margin": row_margin, "column_coupling": column_coupling, "row_coupling": row_coupling, "column_target": column_target, "row_target": row_target, "column_source": column_source, "row_source": row_source, "column_sends": column_sends, "row_sends": row_sends, "term_counts": term_counts}


def term_sources(sources, sends, along_column):
    term_ids = jnp.arange(TERMS, dtype=jnp.int32)
    device = term_ids // TERMS_DEV
    first = device // N_OJ
    second = device % N_OJ
    source_peer = sources // CAP
    position = sources % CAP
    if along_column:
        sender = source_peer * N_OJ + second
        list_row = sender * N_OI + first
    else:
        sender = first * N_OJ + source_peer
        list_row = sender * N_OJ + second
    local_pair = sends[list_row.astype(jnp.int32), position.astype(jnp.int32)]
    return (sender * PAIRS_DEV + local_pair).astype(jnp.int32)


def term_weights(coupling, live_counts):
    term_ids = jnp.arange(TERMS, dtype=jnp.int32)
    device = term_ids // TERMS_DEV
    live_mask = (term_ids % TERMS_DEV) < live_counts[device]
    return jnp.where(live_mask, coupling, jnp.zeros_like(coupling))


def coupled(frozen, spare_allowance, source_pairs, weights, targets):
    def one_device(pieces):
        tile_slack_limit, block_sources, block_weights, block_targets = pieces
        tile_partitions = frozen[block_sources]
        central_split_index = jnp.einsum("ldq,lqp->ldp", tile_slack_limit.astype(jnp.float32), tile_partitions.astype(jnp.float32)).astype(jnp.bfloat16)
        congruent_projection = jnp.einsum("nlu,nyu->nly", central_split_index.astype(jnp.float32), tile_slack_limit.astype(jnp.float32))
        return jax.ops.segment_sum(congruent_projection * block_weights[:, None, None], block_targets, num_segments=PAIRS_DEV)

    devices_total = TERMS // TERMS_DEV
    result = lax.map(one_device, (spare_allowance.reshape(devices_total, TERMS_DEV, PNO, PNO),
                                  source_pairs.reshape(devices_total, TERMS_DEV),
                                  weights.reshape(devices_total, TERMS_DEV),
                                  targets.reshape(devices_total, TERMS_DEV)))
    return result.reshape(PAIRS, PNO, PNO)


def reference(amplitudes, integrals, pno_energy, pair_shift, column_margin, row_margin, column_coupling, row_coupling, column_target, row_target, column_source, row_source, column_sends, row_sends, term_counts):
    orbital_gap_divisor = pno_energy[:, :, None] + pno_energy[:, None, :] + pair_shift[:, None, None]
    column_pair = term_sources(column_source, column_sends, True)
    row_pair = term_sources(row_source, row_sends, False)
    column_weight = term_weights(column_coupling, term_counts[:, 0])
    row_weight = term_weights(row_coupling, term_counts[:, 1])
    residual = integrals
    for relaxation_round in range(ITERS):
        frozen = amplitudes.astype(jnp.bfloat16)
        column_coupled = coupled(frozen, column_margin, column_pair, column_weight, column_target)
        row_coupled = coupled(frozen, row_margin, row_pair, row_weight, row_target)
        residual = integrals + orbital_gap_divisor * amplitudes + column_coupled + row_coupled
        amplitudes = amplitudes - residual / orbital_gap_divisor
    return amplitudes, residual
```

```python
import functools

import jax
import jax.numpy as jnp
from jax import lax
from jax.experimental import pallas as pl
from jax.experimental.pallas import tpu as pltpu
from jax.sharding import PartitionSpec as P

ITERS = 2
CHUNK = 16
GROUP = 4
UNROLL = 18
AXES = ("oi", "oj")
MESH = pl.DeviceIdType.MESH


def partner(index, k, size):
    if size & (size - 1):
        return lax.rem(index + k, size)
    flipped = index
    bit = 1
    while bit < size:
        if k & bit:
            flipped = flipped + bit - 2 * bit * lax.rem(index // bit, 2)
        bit *= 2
    return flipped


def slot_count(terms, pairs):
    step = GROUP * UNROLL
    return -(-(terms + pairs * (GROUP - 1)) // step) * step


def arrange(coupling, target, source, live, pairs):
    terms = coupling.shape[0]
    slots = -(-slot_count(terms, pairs) // 128) * 128
    term_ids = jnp.arange(terms, dtype=jnp.int32)
    weight = jnp.where(term_ids < live, coupling, 0.0)
    same = (target[:, None] == target[None, :]) & (term_ids[:, None] > term_ids[None, :])
    rank = jnp.sum(same.astype(jnp.int32), axis=1)
    pair_ids = jnp.arange(pairs, dtype=jnp.int32)
    member = (target[:, None] == pair_ids[None, :]).astype(jnp.int32)
    groups = (jnp.sum(member, axis=0) + GROUP - 1) // GROUP
    before = jnp.sum(jnp.where(pair_ids[None, :] < pair_ids[:, None], groups[None, :], 0), axis=1)
    base = jnp.sum(member * before[None, :], axis=1) * GROUP
    slot = base + rank
    slot_ids = jnp.arange(slots, dtype=jnp.int32)
    hot = slot[None, :] == slot_ids[:, None]

    def place(values):
        return jnp.sum(jnp.where(hot, values[None, :], jnp.zeros_like(values)[None, :]), axis=1)

    return place(weight), place(term_ids), place(source), place(target)


def jacobi_kernel(
    sizes,
    amplitudes_hbm,
    integrals_hbm,
    pno_energy_hbm,
    pair_shift_hbm,
    column_margin,
    row_margin,
    weights_hbm,
    orders_hbm,
    sources_hbm,
    targets_hbm,
    column_sends_hbm,
    row_sends_hbm,
    latest_hbm,
    total_hbm,
    amplitudes,
    integrals,
    pno_energy,
    pair_shift,
    weights,
    orders,
    sources,
    targets,
    column_sends,
    row_sends,
    margins,
    total,
    frozen,
    column_out,
    row_out,
    column_first,
    row_first,
    column_later,
    row_later,
    input_sems,
    margin_sems,
    column_send_sems,
    column_recv_sems,
    row_send_sems,
    row_recv_sems,
    output_sems,
):
    pairs, width = pno_energy.shape
    terms = margins.shape[1]
    cap = column_out.shape[2]
    chunks = terms // CHUNK
    me = [lax.axis_index(axis) for axis in AXES]
    margin_refs = (column_margin, row_margin)
    sends = (column_sends, row_sends)
    outs = (column_out, row_out)
    ins = ((column_first, row_first), (column_later, row_later))
    send_sems = (column_send_sems, row_send_sems)
    recv_sems = (column_recv_sems, row_recv_sems)

    staged = (
        (column_sends_hbm, column_sends),
        (row_sends_hbm, row_sends),
        (amplitudes_hbm, amplitudes),
        (weights_hbm, weights),
        (orders_hbm, orders),
        (sources_hbm, sources),
        (targets_hbm, targets),
        (pair_shift_hbm, pair_shift),
        (pno_energy_hbm, pno_energy),
        (integrals_hbm, integrals),
    )
    stage_copies = [
        pltpu.make_async_copy(source, target, input_sems.at[i])
        for i, (source, target) in enumerate(staged)
    ]
    for copy in stage_copies:
        copy.start()

    barrier = pltpu.get_barrier_semaphore()
    for side in range(2):
        for k in range(1, sizes[side]):
            peer = partner(me[side], k, sizes[side])
            pl.semaphore_signal(
                barrier, inc=1, device_id={AXES[side]: peer}, device_id_type=MESH
            )

    def fetch(side, chunk):
        part = pl.ds(chunk * CHUNK, CHUNK)
        return pltpu.make_async_copy(
            margin_refs[side].at[part], margins.at[side, part], margin_sems.at[side, chunk]
        )

    for side in range(2):
        for chunk in range(chunks):
            fetch(side, chunk).start()

    for copy in stage_copies[:3]:
        copy.wait()
    for p in range(pairs):
        frozen[p] = amplitudes[p].astype(jnp.bfloat16)

    def exchange(sweep, side, k):
        peer = partner(me[side], k, sizes[side])
        return pltpu.make_async_remote_copy(
            src_ref=outs[side].at[sweep, k],
            dst_ref=ins[sweep][side].at[pl.ds(me[side] * cap, cap)],
            send_sem=send_sems[side].at[sweep, k],
            recv_sem=recv_sems[side].at[sweep, k],
            device_id={AXES[side]: peer},
            device_id_type=MESH,
        )

    def pack(sweep, side):
        for k in range(sizes[side]):
            peer = partner(me[side], k, sizes[side])
            for c in range(cap):
                block = frozen[sends[side][c, peer]]
                if k == 0:
                    ins[sweep][side][me[side] * cap + c] = block
                else:
                    outs[side][sweep, k, c] = block

    def launch(sweep):
        for side in (1, 0):
            pack(sweep, side)
            if sweep == 0 and side == 1:
                pl.semaphore_wait(barrier, sizes[0] + sizes[1] - 2)
            for k in reversed(range(1, sizes[side])):
                exchange(sweep, side, k).start()

    slots = slot_count(terms, pairs)

    def couple(sweep, side):
        blocks = ins[sweep][side]

        def step(index, carry):
            for u in range(UNROLL):
                first = (index * UNROLL + u) * GROUP
                slot = [first + i for i in range(GROUP)]
                margin = [margins[side, orders[side, i]] for i in slot]
                block = [blocks[sources[side, i]] for i in slot]
                halves = []
                for i in range(0, GROUP, 2):
                    empty = jnp.zeros_like(block[i])
                    both = jnp.concatenate(
                        [
                            jnp.concatenate([block[i], empty], axis=1),
                            jnp.concatenate([empty, block[i + 1]], axis=1),
                        ],
                        axis=0,
                    )
                    half = jnp.dot(
                        jnp.concatenate(margin[i : i + 2], axis=1),
                        both,
                        preferred_element_type=jnp.float32,
                    )
                    for j in range(2):
                        part = half[:, j * width : (j + 1) * width]
                        halves.append((part * weights[side, slot[i + j]]).astype(jnp.bfloat16))
                whole = lax.dot_general(
                    jnp.concatenate(halves, axis=1),
                    jnp.concatenate(margin, axis=1),
                    (((1,), (1,)), ((), ())),
                    preferred_element_type=jnp.float32,
                )
                target = targets[side, first]
                for p in range(pairs):
                    total[p] += whole * jnp.where(target == p, 1.0, 0.0)
            return carry

        lax.fori_loop(0, slots // (GROUP * UNROLL), step, 0)

    for sweep in range(ITERS):
        launch(sweep)
        total[...] = jnp.zeros_like(total)
        if sweep == 0:
            for copy in stage_copies[3:]:
                copy.wait()
            for side in range(2):
                for chunk in range(chunks):
                    fetch(side, chunk).wait()
        for side in range(2):
            for k in range(1, sizes[side]):
                exchange(sweep, side, k).wait_recv()
            couple(sweep, side)
        for p in range(pairs if sweep < ITERS - 1 else 0):
            across = jnp.broadcast_to(pno_energy[p : p + 1, :], (width, width))
            divisor = across.T + across + pair_shift[p]
            old = amplitudes[p]
            rest = integrals[p] + divisor * old + total[p]
            new = old - rest / divisor
            frozen[p] = new.astype(jnp.bfloat16)
            amplitudes[p] = new

    results = (
        pltpu.make_async_copy(amplitudes, latest_hbm, output_sems.at[0]),
        pltpu.make_async_copy(total, total_hbm, output_sems.at[1]),
    )
    for copy in results:
        copy.start()
    for sweep in range(ITERS):
        for side in range(2):
            for k in range(1, sizes[side]):
                exchange(sweep, side, k).wait_send()
    for copy in results:
        copy.wait()


def shards(sizes, *operands):
    counts = operands[14]
    pairs = operands[0].shape[0]
    couplings, targets, sources = (jnp.stack(operands[i : i + 2]) for i in (6, 8, 10))
    arranged = jax.vmap(functools.partial(arrange, pairs=pairs))(
        couplings, targets, sources, counts[0]
    )
    operands = operands[:6] + arranged + (operands[12].T, operands[13].T)
    amplitudes, pno_energy, column_margin = operands[0], operands[2], operands[4]
    column_sends = operands[10]
    terms, width, _ = column_margin.shape
    cap = column_sends.shape[0]
    hbm = pl.BlockSpec(memory_space=pltpu.HBM)
    in_vmem = (0, 1, 2)
    in_smem = (3,) + tuple(range(6, 12))

    def held(i, space):
        return space(operands[i].shape, operands[i].dtype)

    def buffer(*shape):
        return pltpu.VMEM(shape + (width, width), jnp.bfloat16)

    dma = pltpu.SemaphoreType.DMA
    latest, coupled = pl.pallas_call(
            functools.partial(jacobi_kernel, sizes),
            out_shape=[jax.ShapeDtypeStruct(amplitudes.shape, jnp.float32)] * 2,
            in_specs=[hbm] * len(operands),
            out_specs=[hbm] * 2,
            scratch_shapes=[held(i, pltpu.VMEM) for i in in_vmem]
            + [held(i, pltpu.SMEM) for i in in_smem]
            + [
                buffer(2, terms),
                pltpu.VMEM(amplitudes.shape, jnp.float32),
                buffer(amplitudes.shape[0]),
                buffer(ITERS, sizes[0], cap),
                buffer(ITERS, sizes[1], cap),
            ]
            + [buffer(size * cap) for size in sizes] * ITERS
            + [
                dma((len(in_vmem) + len(in_smem),)),
                dma((2, terms // CHUNK)),
                dma((ITERS, sizes[0])),
                dma((ITERS, sizes[0])),
                dma((ITERS, sizes[1])),
                dma((ITERS, sizes[1])),
                dma((2,)),
            ],
            compiler_params=pltpu.CompilerParams(
                collective_id=0,
                has_side_effects=True,
            ),
            name="jacobi",
        )(*operands)
    integrals, pair_shift = operands[1], operands[3]
    divisor = pno_energy[:, :, None] + pno_energy[:, None, :] + pair_shift[:, None, None]
    residual = integrals + divisor * latest + coupled
    return (latest - residual / divisor, residual)


def solution(mesh):
    sizes = tuple(mesh.shape[axis] for axis in AXES)
    in_specs = (
        (P(AXES, None, None),) * 2
        + (P(AXES, None), P(AXES))
        + (P(AXES, None, None),) * 2
        + (P(AXES),) * 6
        + (P(AXES, None),) * 3
    )
    out_specs = (P(AXES, None, None), P(AXES, None, None))
    return jax.shard_map(
        functools.partial(shards, sizes),
        mesh=mesh,
        in_specs=in_specs,
        out_specs=out_specs,
        check_vma=False,
    )
```

```python
import functools

import jax
import jax.numpy as jnp
from jax import lax
from jax.experimental import pallas as pl
from jax.experimental.pallas import tpu as pltpu
from jax.sharding import PartitionSpec as P

ITERS = 2
CHUNK = 16
GROUP = 4
UNROLL = 18
AXES = ("oi", "oj")
MESH = pl.DeviceIdType.MESH


def partner(index, k, size):
    if size & (size - 1):
        return lax.rem(index + k, size)
    flipped = index
    bit = 1
    while bit < size:
        if k & bit:
            flipped = flipped + bit - 2 * bit * lax.rem(index // bit, 2)
        bit *= 2
    return flipped


def relayed(size):
    return size >= 8 and not size & (size - 1)


def slot_count(terms, pairs):
    step = GROUP * UNROLL
    return -(-(terms + pairs * (GROUP - 1)) // step) * step


def arrange(coupling, target, source, live, pairs):
    terms = coupling.shape[0]
    slots = -(-slot_count(terms, pairs) // 128) * 128
    term_ids = jnp.arange(terms, dtype=jnp.int32)
    weight = jnp.where(term_ids < live, coupling, 0.0)
    same = (target[:, None] == target[None, :]) & (term_ids[:, None] > term_ids[None, :])
    rank = jnp.sum(same.astype(jnp.int32), axis=1)
    pair_ids = jnp.arange(pairs, dtype=jnp.int32)
    member = (target[:, None] == pair_ids[None, :]).astype(jnp.int32)
    groups = (jnp.sum(member, axis=0) + GROUP - 1) // GROUP
    before = jnp.sum(jnp.where(pair_ids[None, :] < pair_ids[:, None], groups[None, :], 0), axis=1)
    base = jnp.sum(member * before[None, :], axis=1) * GROUP
    slot = base + rank
    slot_ids = jnp.arange(slots, dtype=jnp.int32)
    hot = slot[None, :] == slot_ids[:, None]

    def place(values):
        return jnp.sum(jnp.where(hot, values[None, :], jnp.zeros_like(values)[None, :]), axis=1)

    return place(weight), place(term_ids), place(source), place(target)


def jacobi_kernel(
    sizes,
    amplitudes_hbm,
    integrals_hbm,
    pno_energy_hbm,
    pair_shift_hbm,
    column_margin,
    row_margin,
    weights_hbm,
    orders_hbm,
    sources_hbm,
    targets_hbm,
    column_sends_hbm,
    row_sends_hbm,
    latest_hbm,
    total_hbm,
    amplitudes,
    integrals,
    pno_energy,
    pair_shift,
    weights,
    orders,
    sources,
    targets,
    column_sends,
    row_sends,
    margins,
    total,
    frozen,
    column_out,
    row_out,
    column_first,
    row_first,
    column_later,
    row_later,
    whole_first,
    whole_later,
    table_in,
    table,
    input_sems,
    margin_sems,
    column_send_sems,
    column_recv_sems,
    row_send_sems,
    row_recv_sems,
    whole_sems,
    table_sems,
    output_sems,
):
    pairs, width = pno_energy.shape
    terms = margins.shape[1]
    cap = column_out.shape[2]
    chunks = terms // CHUNK
    me = [lax.axis_index(axis) for axis in AXES]
    margin_refs = (column_margin, row_margin)
    sends = (column_sends, row_sends)
    outs = (column_out, row_out)
    ins = ((column_first, row_first), (column_later, row_later))
    send_sems = (column_send_sems, row_send_sems)
    recv_sems = (column_recv_sems, row_recv_sems)

    staged = (
        (column_sends_hbm, column_sends),
        (row_sends_hbm, row_sends),
        (amplitudes_hbm, amplitudes),
        (weights_hbm, weights),
        (orders_hbm, orders),
        (sources_hbm, sources),
        (targets_hbm, targets),
        (pair_shift_hbm, pair_shift),
        (pno_energy_hbm, pno_energy),
        (integrals_hbm, integrals),
    )
    stage_copies = [
        pltpu.make_async_copy(source, target, input_sems.at[i])
        for i, (source, target) in enumerate(staged)
    ]
    for copy in stage_copies:
        copy.start()

    barrier = pltpu.get_barrier_semaphore()
    for side in range(2):
        for k in range(1, sizes[side]):
            peer = partner(me[side], k, sizes[side])
            pl.semaphore_signal(
                barrier, inc=1, device_id={AXES[side]: peer}, device_id_type=MESH
            )

    def fetch(side, chunk):
        part = pl.ds(chunk * CHUNK, CHUNK)
        return pltpu.make_async_copy(
            margin_refs[side].at[part], margins.at[side, part], margin_sems.at[side, chunk]
        )

    for side in range(2):
        for chunk in range(chunks):
            fetch(side, chunk).start()

    for copy in stage_copies[:3]:
        copy.wait()
    for p in range(pairs):
        frozen[0, p] = amplitudes[p].astype(jnp.bfloat16)

    count = sizes[1]
    relay = relayed(count)
    whole_in = (whole_first, whole_later)
    chip = me[1] // 2
    inner = (chip == count // 4 - 1) | (chip == count // 4)
    opposite = partner(me[1], count - 2, count)
    handed = (count - 4, count - 3, count - 1) if relay else ()

    def send_whole(sweep):
        return pltpu.make_async_remote_copy(
            src_ref=frozen.at[sweep],
            dst_ref=whole_in[sweep],
            send_sem=whole_sems.at[0, sweep],
            recv_sem=whole_sems.at[1, sweep],
            device_id={AXES[1]: opposite},
            device_id_type=MESH,
        )

    def send_table():
        return pltpu.make_async_remote_copy(
            src_ref=row_sends_hbm,
            dst_ref=table_in,
            send_sem=table_sems.at[0],
            recv_sem=table_sems.at[1],
            device_id={AXES[1]: opposite},
            device_id_type=MESH,
        )

    def hand_on(sweep, k):
        peer = partner(opposite, k, count)
        return pltpu.make_async_remote_copy(
            src_ref=outs[1].at[sweep, k],
            dst_ref=ins[sweep][1].at[pl.ds(opposite * cap, cap)],
            send_sem=send_sems[1].at[sweep, k],
            recv_sem=recv_sems[1].at[sweep, k],
            device_id={AXES[1]: peer},
            device_id_type=MESH,
        )

    def exchange(sweep, side, k):
        peer = partner(me[side], k, sizes[side])
        return pltpu.make_async_remote_copy(
            src_ref=outs[side].at[sweep, k],
            dst_ref=ins[sweep][side].at[pl.ds(me[side] * cap, cap)],
            send_sem=send_sems[side].at[sweep, k],
            recv_sem=recv_sems[side].at[sweep, k],
            device_id={AXES[side]: peer},
            device_id_type=MESH,
        )

    def pack(sweep, side, k):
        peer = partner(me[side], k, sizes[side])
        for c in range(cap):
            block = frozen[sweep, sends[side][c, peer]]
            if k == 0:
                ins[sweep][side][me[side] * cap + c] = block
            else:
                outs[side][sweep, k, c] = block

    def send(sweep, side, k):
        pack(sweep, side, k)
        exchange(sweep, side, k).start()

    def launch(sweep):
        if sweep == 0:
            pl.semaphore_wait(barrier, sizes[0] + sizes[1] - 2)
        if relay:

            @pl.when(inner)
            def _():
                send_whole(sweep).start()
                if sweep == 0:
                    send_table().start()

        near = [k for k in (2, 3) if k < count]
        for k in near:
            send(sweep, 1, k)
        far = [k for k in reversed(range(4, count)) if not relay or k < count - 4]
        for k in far:
            send(sweep, 1, k)
        if relay:

            @pl.when(jnp.logical_not(inner))
            def _():
                for k in (count - 2, count - 1, count - 4, count - 3):
                    send(sweep, 1, k)

        if count > 1:
            send(sweep, 1, 1)
        for k in reversed(range(1, sizes[0])):
            send(sweep, 0, k)
        for side in range(2):
            pack(sweep, side, 0)

    def pass_on(sweep):
        if relay:

            @pl.when(inner)
            def _():
                if sweep == 0:
                    send_table().wait_recv()
                    lookup = pltpu.make_async_copy(table_in, table, table_sems.at[2])
                    lookup.start()
                    lookup.wait()
                send_whole(sweep).wait_recv()
                for k in handed:
                    peer = partner(opposite, k, count)
                    for c in range(cap):
                        outs[1][sweep, k, c] = whole_in[sweep][table[c, peer]]
                    hand_on(sweep, k).start()
                for c in range(cap):
                    ins[sweep][1][opposite * cap + c] = whole_in[sweep][table[c, me[1]]]

    def received(sweep, side):
        for k in range(1, sizes[side]):
            if side == 1 and relay and k == count - 2:

                @pl.when(jnp.logical_not(inner))
                def _():
                    exchange(sweep, side, k).wait_recv()

            else:
                exchange(sweep, side, k).wait_recv()

    def sent(sweep, side):
        for k in range(1, sizes[side]):
            if side == 1 and relay and k == count - 2:

                @pl.when(jnp.logical_not(inner))
                def _():
                    exchange(sweep, side, k).wait_send()

                @pl.when(inner)
                def _():
                    send_whole(sweep).wait_send()
                    if sweep == 0:
                        send_table().wait_send()

            else:
                exchange(sweep, side, k).wait_send()

    slots = slot_count(terms, pairs)

    def couple(sweep, side):
        blocks = ins[sweep][side]

        def step(index, carry):
            for u in range(UNROLL):
                first = (index * UNROLL + u) * GROUP
                slot = [first + i for i in range(GROUP)]
                margin = [margins[side, orders[side, i]] for i in slot]
                block = [blocks[sources[side, i]] for i in slot]
                halves = []
                for i in range(0, GROUP, 2):
                    empty = jnp.zeros_like(block[i])
                    both = jnp.concatenate(
                        [
                            jnp.concatenate([block[i], empty], axis=1),
                            jnp.concatenate([empty, block[i + 1]], axis=1),
                        ],
                        axis=0,
                    )
                    half = jnp.dot(
                        jnp.concatenate(margin[i : i + 2], axis=1),
                        both,
                        preferred_element_type=jnp.float32,
                    )
                    for j in range(2):
                        part = half[:, j * width : (j + 1) * width]
                        halves.append((part * weights[side, slot[i + j]]).astype(jnp.bfloat16))
                whole = lax.dot_general(
                    jnp.concatenate(halves, axis=1),
                    jnp.concatenate(margin, axis=1),
                    (((1,), (1,)), ((), ())),
                    preferred_element_type=jnp.float32,
                )
                target = targets[side, first]
                for p in range(pairs):
                    total[p] += whole * jnp.where(target == p, 1.0, 0.0)
            return carry

        lax.fori_loop(0, slots // (GROUP * UNROLL), step, 0)

    for sweep in range(ITERS):
        launch(sweep)
        pass_on(sweep)
        total[...] = jnp.zeros_like(total)
        if sweep == 0:
            for copy in stage_copies[3:]:
                copy.wait()
            for side in range(2):
                for chunk in range(chunks):
                    fetch(side, chunk).wait()
        for side in range(2):
            received(sweep, side)
            couple(sweep, side)
        for p in range(pairs if sweep < ITERS - 1 else 0):
            across = jnp.broadcast_to(pno_energy[p : p + 1, :], (width, width))
            divisor = across.T + across + pair_shift[p]
            old = amplitudes[p]
            rest = integrals[p] + divisor * old + total[p]
            new = old - rest / divisor
            frozen[sweep + 1, p] = new.astype(jnp.bfloat16)
            amplitudes[p] = new

    results = (
        pltpu.make_async_copy(amplitudes, latest_hbm, output_sems.at[0]),
        pltpu.make_async_copy(total, total_hbm, output_sems.at[1]),
    )
    for copy in results:
        copy.start()
    for sweep in range(ITERS):
        for side in range(2):
            sent(sweep, side)
    for copy in results:
        copy.wait()


def shards(sizes, *operands):
    counts = operands[14]
    pairs = operands[0].shape[0]
    couplings, targets, sources = (jnp.stack(operands[i : i + 2]) for i in (6, 8, 10))
    arranged = jax.vmap(functools.partial(arrange, pairs=pairs))(
        couplings, targets, sources, counts[0]
    )
    operands = operands[:6] + arranged + (operands[12].T, operands[13].T)
    amplitudes, pno_energy, column_margin = operands[0], operands[2], operands[4]
    column_sends = operands[10]
    terms, width, _ = column_margin.shape
    cap = column_sends.shape[0]
    hbm = pl.BlockSpec(memory_space=pltpu.HBM)
    in_vmem = (0, 1, 2)
    in_smem = (3,) + tuple(range(6, 12))

    def held(i, space):
        return space(operands[i].shape, operands[i].dtype)

    def buffer(*shape):
        return pltpu.VMEM(shape + (width, width), jnp.bfloat16)

    dma = pltpu.SemaphoreType.DMA
    latest, coupled = pl.pallas_call(
            functools.partial(jacobi_kernel, sizes),
            out_shape=[jax.ShapeDtypeStruct(amplitudes.shape, jnp.float32)] * 2,
            in_specs=[hbm] * len(operands),
            out_specs=[hbm] * 2,
            scratch_shapes=[held(i, pltpu.VMEM) for i in in_vmem]
            + [held(i, pltpu.SMEM) for i in in_smem]
            + [
                buffer(2, terms),
                pltpu.VMEM(amplitudes.shape, jnp.float32),
                buffer(ITERS, amplitudes.shape[0]),
                buffer(ITERS, sizes[0], cap),
                buffer(ITERS, sizes[1], cap),
            ]
            + [buffer(size * cap) for size in sizes] * ITERS
            + [buffer(amplitudes.shape[0])] * ITERS
            + [
                held(11, pltpu.VMEM),
                held(11, pltpu.SMEM),
            ]
            + [
                dma((len(in_vmem) + len(in_smem),)),
                dma((2, terms // CHUNK)),
                dma((ITERS, sizes[0])),
                dma((ITERS, sizes[0])),
                dma((ITERS, sizes[1])),
                dma((ITERS, sizes[1])),
                dma((2, ITERS)),
                dma((3,)),
                dma((2,)),
            ],
            compiler_params=pltpu.CompilerParams(
                collective_id=0,
                has_side_effects=True,
            ),
            name="jacobi",
        )(*operands)
    integrals, pair_shift = operands[1], operands[3]
    divisor = pno_energy[:, :, None] + pno_energy[:, None, :] + pair_shift[:, None, None]
    residual = integrals + divisor * latest + coupled
    return (latest - residual / divisor, residual)


def solution(mesh):
    sizes = tuple(mesh.shape[axis] for axis in AXES)
    in_specs = (
        (P(AXES, None, None),) * 2
        + (P(AXES, None), P(AXES))
        + (P(AXES, None, None),) * 2
        + (P(AXES),) * 6
        + (P(AXES, None),) * 3
    )
    out_specs = (P(AXES, None, None), P(AXES, None, None))
    return jax.shard_map(
        functools.partial(shards, sizes),
        mesh=mesh,
        in_specs=in_specs,
        out_specs=out_specs,
        check_vma=False,
    )
```

```python
import functools

import jax
import jax.numpy as jnp
from jax import lax
from jax.experimental import pallas as pl
from jax.experimental.pallas import tpu as pltpu
from jax.sharding import PartitionSpec as P

ITERS = 2
CHUNK = 16
GROUP = 4
UNROLL = 18
AXES = ("oi", "oj")
MESH = pl.DeviceIdType.MESH


def partner(index, k, size):
    if size & (size - 1):
        return lax.rem(index + k, size)
    flipped = index
    bit = 1
    while bit < size:
        if k & bit:
            flipped = flipped + bit - 2 * bit * lax.rem(index // bit, 2)
        bit *= 2
    return flipped


def relayed(size):
    return size >= 8 and not size & (size - 1)


def slot_count(terms, pairs):
    step = GROUP * UNROLL
    return -(-(terms + pairs * (GROUP - 1)) // step) * step


def arrange(coupling, target, source, live, pairs, slots):
    terms = target.shape[1]
    square = (terms, terms)

    def column(row):
        return jnp.broadcast_to(row, square).T

    def total_of(mask, values):
        return jnp.sum(jnp.where(mask, values, jnp.zeros_like(values)), axis=0, keepdims=True)

    down = lax.broadcasted_iota(jnp.int32, square, 0)
    across = lax.broadcasted_iota(jnp.int32, square, 1)
    ones = jnp.ones(square, jnp.int32)
    weight = jnp.where(across[:1] < live, coupling, 0.0)
    target_column = column(target)
    rank = total_of((target_column == target) & (down < across), ones)
    base = jnp.zeros_like(target)
    start = jnp.zeros_like(target)
    for p in range(pairs):
        base = jnp.where(target == p, start, base)
        start = start + ((total_of(target_column == p, ones) + GROUP - 1) & -GROUP)
    slot = column(base + rank)
    columns = (column(weight), down, column(source), target_column)
    placed = []
    for values in columns:
        parts = [total_of(slot == across + first, values) for first in range(0, slots, terms)]
        placed.append(jnp.concatenate(parts, axis=1))
    return placed


def jacobi_kernel(
    sizes,
    amplitudes_hbm,
    integrals_hbm,
    pno_energy_hbm,
    pair_shift_hbm,
    column_margin,
    row_margin,
    column_coupling_hbm,
    row_coupling_hbm,
    column_target_hbm,
    row_target_hbm,
    column_source_hbm,
    row_source_hbm,
    column_sends_hbm,
    row_sends_hbm,
    counts_hbm,
    latest_hbm,
    total_hbm,
    amplitudes,
    integrals,
    pno_energy,
    column_coupling,
    row_coupling,
    column_target,
    row_target,
    column_source,
    row_source,
    pair_shift,
    column_sends,
    row_sends,
    counts,
    arranged_weights,
    arranged_orders,
    arranged_sources,
    arranged_targets,
    weights,
    orders,
    sources,
    targets,
    margins,
    total,
    frozen,
    column_out,
    row_out,
    column_first,
    row_first,
    column_later,
    row_later,
    whole_first,
    whole_later,
    table_in,
    table,
    input_sems,
    place_sems,
    margin_sems,
    column_send_sems,
    column_recv_sems,
    row_send_sems,
    row_recv_sems,
    whole_sems,
    table_sems,
    output_sems,
):
    pairs, width = pno_energy.shape
    terms = margins.shape[1]
    cap = column_out.shape[2]
    chunks = terms // CHUNK
    me = [lax.axis_index(axis) for axis in AXES]
    margin_refs = (column_margin, row_margin)
    sends = (column_sends, row_sends)
    outs = (column_out, row_out)
    ins = ((column_first, row_first), (column_later, row_later))
    send_sems = (column_send_sems, row_send_sems)
    recv_sems = (column_recv_sems, row_recv_sems)

    staged = (
        (column_sends_hbm, column_sends),
        (row_sends_hbm, row_sends),
        (amplitudes_hbm, amplitudes),
        (counts_hbm, counts),
        (column_coupling_hbm, column_coupling),
        (row_coupling_hbm, row_coupling),
        (column_target_hbm, column_target),
        (row_target_hbm, row_target),
        (column_source_hbm, column_source),
        (row_source_hbm, row_source),
        (pair_shift_hbm, pair_shift),
        (pno_energy_hbm, pno_energy),
        (integrals_hbm, integrals),
    )
    stage_copies = [
        pltpu.make_async_copy(source, target, input_sems.at[i])
        for i, (source, target) in enumerate(staged)
    ]
    for copy in stage_copies:
        copy.start()

    barrier = pltpu.get_barrier_semaphore()
    for side in range(2):
        for k in range(1, sizes[side]):
            peer = partner(me[side], k, sizes[side])
            pl.semaphore_signal(
                barrier, inc=1, device_id={AXES[side]: peer}, device_id_type=MESH
            )

    def fetch(side, chunk):
        part = pl.ds(chunk * CHUNK, CHUNK)
        return pltpu.make_async_copy(
            margin_refs[side].at[part], margins.at[side, part], margin_sems.at[side, chunk]
        )

    for side in range(2):
        for chunk in range(chunks):
            fetch(side, chunk).start()

    for copy in stage_copies[:3]:
        copy.wait()
    for p in range(pairs):
        frozen[0, p] = amplitudes[p].astype(jnp.bfloat16)

    count = sizes[1]
    relay = relayed(count)
    whole_in = (whole_first, whole_later)
    chip = me[1] // 2
    inner = (chip == count // 4 - 1) | (chip == count // 4)
    opposite = partner(me[1], count - 2, count)
    handed = (count - 4, count - 3, count - 1) if relay else ()

    def send_whole(sweep):
        return pltpu.make_async_remote_copy(
            src_ref=frozen.at[sweep],
            dst_ref=whole_in[sweep],
            send_sem=whole_sems.at[0, sweep],
            recv_sem=whole_sems.at[1, sweep],
            device_id={AXES[1]: opposite},
            device_id_type=MESH,
        )

    def send_table():
        return pltpu.make_async_remote_copy(
            src_ref=row_sends_hbm,
            dst_ref=table_in,
            send_sem=table_sems.at[0],
            recv_sem=table_sems.at[1],
            device_id={AXES[1]: opposite},
            device_id_type=MESH,
        )

    def hand_on(sweep, k):
        peer = partner(opposite, k, count)
        return pltpu.make_async_remote_copy(
            src_ref=outs[1].at[sweep, k],
            dst_ref=ins[sweep][1].at[pl.ds(opposite * cap, cap)],
            send_sem=send_sems[1].at[sweep, k],
            recv_sem=recv_sems[1].at[sweep, k],
            device_id={AXES[1]: peer},
            device_id_type=MESH,
        )

    def exchange(sweep, side, k):
        peer = partner(me[side], k, sizes[side])
        return pltpu.make_async_remote_copy(
            src_ref=outs[side].at[sweep, k],
            dst_ref=ins[sweep][side].at[pl.ds(me[side] * cap, cap)],
            send_sem=send_sems[side].at[sweep, k],
            recv_sem=recv_sems[side].at[sweep, k],
            device_id={AXES[side]: peer},
            device_id_type=MESH,
        )

    def pack(sweep, side, k):
        peer = partner(me[side], k, sizes[side])
        for c in range(cap):
            block = frozen[sweep, sends[side][c, peer]]
            if k == 0:
                ins[sweep][side][me[side] * cap + c] = block
            else:
                outs[side][sweep, k, c] = block

    def send(sweep, side, k):
        pack(sweep, side, k)
        exchange(sweep, side, k).start()

    def launch(sweep):
        if sweep == 0:
            pl.semaphore_wait(barrier, sizes[0] + sizes[1] - 2)
        if relay:

            @pl.when(inner)
            def _():
                send_whole(sweep).start()
                if sweep == 0:
                    send_table().start()

        near = [k for k in (2, 3) if k < count]
        for k in near:
            send(sweep, 1, k)
        far = [k for k in reversed(range(4, count)) if not relay or k < count - 4]
        for k in far:
            send(sweep, 1, k)
        if relay:

            @pl.when(jnp.logical_not(inner))
            def _():
                for k in (count - 2, count - 1, count - 4, count - 3):
                    send(sweep, 1, k)

        if count > 1:
            send(sweep, 1, 1)
        for k in reversed(range(1, sizes[0])):
            send(sweep, 0, k)
        for side in range(2):
            pack(sweep, side, 0)

    def pass_on(sweep):
        if relay:

            @pl.when(inner)
            def _():
                if sweep == 0:
                    send_table().wait_recv()
                    lookup = pltpu.make_async_copy(table_in, table, table_sems.at[2])
                    lookup.start()
                    lookup.wait()
                send_whole(sweep).wait_recv()
                for k in handed:
                    peer = partner(opposite, k, count)
                    for c in range(cap):
                        outs[1][sweep, k, c] = whole_in[sweep][table[c, peer]]
                    hand_on(sweep, k).start()
                for c in range(cap):
                    ins[sweep][1][opposite * cap + c] = whole_in[sweep][table[c, me[1]]]

    def received(sweep, side):
        for k in range(1, sizes[side]):
            if side == 1 and relay and k == count - 2:

                @pl.when(jnp.logical_not(inner))
                def _():
                    exchange(sweep, side, k).wait_recv()

            else:
                exchange(sweep, side, k).wait_recv()

    def sent(sweep, side):
        for k in range(1, sizes[side]):
            if side == 1 and relay and k == count - 2:

                @pl.when(jnp.logical_not(inner))
                def _():
                    exchange(sweep, side, k).wait_send()

                @pl.when(inner)
                def _():
                    send_whole(sweep).wait_send()
                    if sweep == 0:
                        send_table().wait_send()

            else:
                exchange(sweep, side, k).wait_send()

    slots = slot_count(terms, pairs)

    def couple(sweep, side):
        blocks = ins[sweep][side]

        def step(index, carry):
            for u in range(UNROLL):
                first = (index * UNROLL + u) * GROUP
                slot = [first + i for i in range(GROUP)]
                margin = [margins[side, orders[side, i]] for i in slot]
                block = [blocks[sources[side, i]] for i in slot]
                halves = []
                for i in range(0, GROUP, 2):
                    empty = jnp.zeros_like(block[i])
                    both = jnp.concatenate(
                        [
                            jnp.concatenate([block[i], empty], axis=1),
                            jnp.concatenate([empty, block[i + 1]], axis=1),
                        ],
                        axis=0,
                    )
                    half = jnp.dot(
                        jnp.concatenate(margin[i : i + 2], axis=1),
                        both,
                        preferred_element_type=jnp.float32,
                    )
                    for j in range(2):
                        part = half[:, j * width : (j + 1) * width]
                        halves.append((part * weights[side, slot[i + j]]).astype(jnp.bfloat16))
                whole = lax.dot_general(
                    jnp.concatenate(halves, axis=1),
                    jnp.concatenate(margin, axis=1),
                    (((1,), (1,)), ((), ())),
                    preferred_element_type=jnp.float32,
                )
                target = targets[side, first]
                for p in range(pairs):
                    total[p] += whole * jnp.where(target == p, 1.0, 0.0)
            return carry

        lax.fori_loop(0, slots // (GROUP * UNROLL), step, 0)

    for sweep in range(ITERS):
        launch(sweep)
        if sweep == 0:
            for copy in stage_copies[3:10]:
                copy.wait()
            terms_in = (
                (column_coupling, column_target, column_source),
                (row_coupling, row_target, row_source),
            )
            staging = (arranged_weights, arranged_orders, arranged_sources, arranged_targets)
            for side in range(2):
                coupling, target, source = terms_in[side]
                rows = arrange(
                    coupling[...],
                    target[...],
                    source[...],
                    counts[0, side],
                    pairs,
                    weights.shape[1],
                )
                for stage, row in zip(staging, rows):
                    stage[side : side + 1, :] = row
            settled = (weights, orders, sources, targets)
            placements = [
                pltpu.make_async_copy(stage, settled[i], place_sems.at[i])
                for i, stage in enumerate(staging)
            ]
            for copy in placements:
                copy.start()
        pass_on(sweep)
        total[...] = jnp.zeros_like(total)
        if sweep == 0:
            for copy in stage_copies[10:] + placements:
                copy.wait()
            for side in range(2):
                for chunk in range(chunks):
                    fetch(side, chunk).wait()
        for side in range(2):
            received(sweep, side)
            couple(sweep, side)
        for p in range(pairs if sweep < ITERS - 1 else 0):
            across = jnp.broadcast_to(pno_energy[p : p + 1, :], (width, width))
            divisor = across.T + across + pair_shift[p]
            old = amplitudes[p]
            rest = integrals[p] + divisor * old + total[p]
            new = old - rest / divisor
            frozen[sweep + 1, p] = new.astype(jnp.bfloat16)
            amplitudes[p] = new

    results = (
        pltpu.make_async_copy(amplitudes, latest_hbm, output_sems.at[0]),
        pltpu.make_async_copy(total, total_hbm, output_sems.at[1]),
    )
    for copy in results:
        copy.start()
    for sweep in range(ITERS):
        for side in range(2):
            sent(sweep, side)
    for copy in results:
        copy.wait()


def shards(sizes, *operands):
    lists = tuple(values.reshape(1, -1) for values in operands[6:12])
    operands = operands[:6] + lists + (operands[12].T, operands[13].T, operands[14])
    amplitudes, pno_energy, column_margin = operands[0], operands[2], operands[4]
    column_sends = operands[12]
    terms, width, _ = column_margin.shape
    cap = column_sends.shape[0]
    slots = -(-slot_count(terms, amplitudes.shape[0]) // terms) * terms
    listed = [(2, slots, jnp.float32)] + [(2, slots, jnp.int32)] * 3
    hbm = pl.BlockSpec(memory_space=pltpu.HBM)
    in_vmem = (0, 1, 2) + tuple(range(6, 12))
    in_smem = (3, 12, 13, 14)

    def held(i, space):
        return space(operands[i].shape, operands[i].dtype)

    def buffer(*shape):
        return pltpu.VMEM(shape + (width, width), jnp.bfloat16)

    dma = pltpu.SemaphoreType.DMA
    latest, coupled = pl.pallas_call(
            functools.partial(jacobi_kernel, sizes),
            out_shape=[jax.ShapeDtypeStruct(amplitudes.shape, jnp.float32)] * 2,
            in_specs=[hbm] * len(operands),
            out_specs=[hbm] * 2,
            scratch_shapes=[held(i, pltpu.VMEM) for i in in_vmem]
            + [held(i, pltpu.SMEM) for i in in_smem]
            + [space((n, m), kind) for space in (pltpu.VMEM, pltpu.SMEM) for n, m, kind in listed]
            + [
                buffer(2, terms),
                pltpu.VMEM(amplitudes.shape, jnp.float32),
                buffer(ITERS, amplitudes.shape[0]),
                buffer(ITERS, sizes[0], cap),
                buffer(ITERS, sizes[1], cap),
            ]
            + [buffer(size * cap) for size in sizes] * ITERS
            + [buffer(amplitudes.shape[0])] * ITERS
            + [
                held(13, pltpu.VMEM),
                held(13, pltpu.SMEM),
            ]
            + [
                dma((len(in_vmem) + len(in_smem),)),
                dma((len(listed),)),
                dma((2, terms // CHUNK)),
                dma((ITERS, sizes[0])),
                dma((ITERS, sizes[0])),
                dma((ITERS, sizes[1])),
                dma((ITERS, sizes[1])),
                dma((2, ITERS)),
                dma((3,)),
                dma((2,)),
            ],
            compiler_params=pltpu.CompilerParams(
                collective_id=0,
                has_side_effects=True,
            ),
            name="jacobi",
        )(*operands)
    integrals, pair_shift = operands[1], operands[3]
    divisor = pno_energy[:, :, None] + pno_energy[:, None, :] + pair_shift[:, None, None]
    residual = integrals + divisor * latest + coupled
    return (latest - residual / divisor, residual)


def solution(mesh):
    sizes = tuple(mesh.shape[axis] for axis in AXES)
    in_specs = (
        (P(AXES, None, None),) * 2
        + (P(AXES, None), P(AXES))
        + (P(AXES, None, None),) * 2
        + (P(AXES),) * 6
        + (P(AXES, None),) * 3
    )
    out_specs = (P(AXES, None, None), P(AXES, None, None))
    return jax.shard_map(
        functools.partial(shards, sizes),
        mesh=mesh,
        in_specs=in_specs,
        out_specs=out_specs,
        check_vma=False,
    )
```
